256 devices in a mesh: gx: 32 (over y, x, core), gy: 8 (over z).
Axes of the slice: x: 4, y: 4, z: 8, core: 2. Of those that a mesh axis runs over, the one named last changes fastest.
Arguments:
- velocity: float32 [2, 10, 3072, 3072], P(None, None, 'gx', 'gy'), may hold values from -6 to 6
- viscosity: float32 [10, 3072, 3072], P(None, 'gx', 'gy'), may hold values from 0.05 to 0.8
- friction: float32 [3072, 3072], P('gx', 'gy'), may hold values from 0.1 to 2
- ice_mask: int32 [32, 8], P('gx', 'gy'), may hold values from 0 to 1, as said below
- obs_tiles: float32 [32, 8, 32, 8, 4, 3, 128], P('gx', 'gy'), as said below
- obs_cell: int32 [32, 8, 32, 8, 4], P('gx', 'gy'), may hold values from 0 to 287, as said below
- obs_count: int32 [32, 8, 32, 8], P('gx', 'gy'), may hold values from 0 to 4, as said below
Outputs:
- adjoint: float32 [2, 10, 3072, 3072], P(None, None, 'gx', 'gy')
- friction_gradient: float32 [3072, 3072], P('gx', 'gy')
The draws below stay inside these ranges and needn't reach their ends.
Inputs may be any that keep to these rules, and one draw needn't show every extreme that they name: `ice_mask`: some block is ice-covered in every draw. `obs_count`: zero for every owner block whose ice_mask is 0; in every draw some owner block receives 4 live tiles from every sending block. `obs_cell`: slots at or beyond the live count also hold anchors in range. `obs_tiles`: channel 2 holds weights between 0.3 and 3.
All inputs are finite; a program needn't handle non-finite values.
Results may differ from the reference program's by a relative error of at most 0.00002.
Values sent between devices are 32-bit elements; how exact they have to be, the bound alone decides.
A program may use at most 128 MiB of HBM per device.

```python
import math
import jax
import jax.numpy as jnp

CX = 96
CY = 384
LAYERS = 10
SWEEPS = 3
TILE = 128
CAP = 4
BLOCKS_X = 32
BLOCKS_Y = 8
NX = 3072
NY = 3072
NB = 3


def ice_and_full(key):
    base = jax.random.fold_in(key, 11)
    first_key, second_key = jax.random.split(base)
    covered = (jax.random.randint(first_key, (BLOCKS_X * BLOCKS_Y,), 0, 4) < 3).astype(jnp.int32)
    full_owner = jax.random.randint(second_key, (), 0, BLOCKS_X * BLOCKS_Y)
    covered = covered.at[full_owner].set(1)
    return (covered.reshape(BLOCKS_X, BLOCKS_Y), full_owner)


def draw_ice_mask(key, part):
    covered, full_owner = ice_and_full(key)
    return covered


def draw_obs_count(key, part):
    covered, full_owner = ice_and_full(key)
    count_key = jax.random.fold_in(key, 12)
    counts = jax.random.randint(count_key, (BLOCKS_X, BLOCKS_Y, BLOCKS_X, BLOCKS_Y), 1, CAP + 1)
    counts = counts * covered[None, None, :, :]
    counts = counts.reshape(BLOCKS_X, BLOCKS_Y, BLOCKS_X * BLOCKS_Y).at[:, :, full_owner].set(CAP)
    return counts.reshape(BLOCKS_X, BLOCKS_Y, BLOCKS_X, BLOCKS_Y).astype(jnp.int32)


def draw_obs_cell(key, part):
    cell_key = jax.random.fold_in(key, 13)
    cells = jax.random.randint(cell_key, (BLOCKS_X * BLOCKS_Y * BLOCKS_X * BLOCKS_Y * CAP,), 0, CX * NB)
    cells = cells.at[0].set(CX * NB - 1).at[1].set(0)
    return cells.reshape(BLOCKS_X, BLOCKS_Y, BLOCKS_X, BLOCKS_Y, CAP).astype(jnp.int32)


def draw_obs_tiles(key, part):
    tile_key = jax.random.fold_in(key, 14)
    u_key, v_key, w_key = jax.random.split(tile_key, 3)
    shape_one = (BLOCKS_X, BLOCKS_Y, BLOCKS_X, BLOCKS_Y, CAP, TILE)
    u_obs = jax.random.normal(u_key, shape_one, jnp.float32)
    v_obs = jax.random.normal(v_key, shape_one, jnp.float32)
    weights = jnp.exp(jax.random.uniform(w_key, shape_one, jnp.float32, jnp.log(0.3), jnp.log(3.0)))
    return jnp.stack([u_obs, v_obs, weights], axis=-2).astype(jnp.float32)


def steps_of(key, dims, cuts, least, top_value):
    factor_of = 1.0
    for axis_at, shards_of in cuts:
        steps = jax.random.uniform(jax.random.fold_in(jax.random.fold_in(key, 6), axis_at), (shards_of,), jnp.float32, least / len(cuts), top_value / len(cuts))
        factor_of = factor_of * jnp.repeat(jnp.exp(steps), dims[axis_at] // shards_of).reshape((-1,) + (1,) * (len(dims) - 1 - axis_at))
    return factor_of


def centred(rng, shape, width, reach, cuts=(), held_as=jnp.bfloat16):
    drawn = jax.random.normal(rng, shape, jnp.float32) * width
    if len(cuts) > 0:
        drawn = steps_of(rng, shape, cuts, -0.22, 0.18) * drawn
    return jnp.clip(drawn, min=-reach, max=reach).astype(held_as)


def setup_inputs(seed: int = 0) -> dict:
    streams_of = jax.random.split(jax.random.key(seed), 8)
    return {
        "velocity": centred(streams_of[0], (2, LAYERS, NX, NY), 1.0, 6.0, ((2, 32), (3, 8)), jnp.float32),
        "viscosity": jnp.clip(jnp.exp(math.log(0.8) - 2.7725887 * jax.random.uniform(streams_of[1], (LAYERS, NX, NY), jnp.float32) ** steps_of(streams_of[1], (LAYERS, NX, NY), ((1, 32), (2, 8)), -0.2, 0.2)), 0.05, 0.8),
        "friction": jnp.clip(jnp.exp(math.log(2.0) - 2.9957323 * jax.random.uniform(streams_of[2], (NX, NY), jnp.float32) ** steps_of(streams_of[2], (NX, NY), ((0, 32), (1, 8)), -0.2, 0.2)), 0.1, 2.0),
        "ice_mask": draw_ice_mask(jax.random.fold_in(streams_of[7], 71), 0),
        "obs_tiles": draw_obs_tiles(jax.random.fold_in(streams_of[7], 71), 0),
        "obs_cell": draw_obs_cell(jax.random.fold_in(streams_of[7], 71), 0),
        "obs_count": draw_obs_count(jax.random.fold_in(streams_of[7], 71), 0),
    }


VERTICAL_GAIN = 2.0
RELAX_WEIGHT = 0.8


def column_factors(padded_visc, friction_field):
    center = padded_visc[:, 1:-1, 1:-1]
    west_face = 0.5 * (center + padded_visc[:, :-2, 1:-1])
    east_face = 0.5 * (center + padded_visc[:, 2:, 1:-1])
    south_face = 0.5 * (center + padded_visc[:, 1:-1, :-2])
    north_face = 0.5 * (center + padded_visc[:, 1:-1, 2:])
    upper_face = VERTICAL_GAIN * 0.5 * (center[:-1] + center[1:])
    layer_count = center.shape[0]
    diagonal = west_face + east_face + south_face + north_face
    pivots = []
    ratios = []
    for level in range(layer_count):
        entry = diagonal[level]
        if level == 0:
            entry = entry + friction_field
        if level < layer_count - 1:
            entry = entry + upper_face[level]
        if level > 0:
            entry = entry + upper_face[level - 1] + upper_face[level - 1] * ratios[level - 1]
        pivots.append(entry)
        if level < layer_count - 1:
            ratios.append(-upper_face[level] / entry)
    return (west_face, east_face, south_face, north_face, upper_face, pivots, ratios)


def relax(padded_adj, rhs_field, factors, icefield):
    west_face, east_face, south_face, north_face, upper_face, pivots, ratios = factors
    center = padded_adj[..., 1:-1, 1:-1]
    driven = rhs_field + west_face * padded_adj[..., :-2, 1:-1] + east_face * padded_adj[..., 2:, 1:-1]
    driven = driven + south_face * padded_adj[..., 1:-1, :-2] + north_face * padded_adj[..., 1:-1, 2:]
    layer_count = len(pivots)
    forward = []
    for level in range(layer_count):
        value = driven[:, level]
        if level > 0:
            value = value + upper_face[level - 1] * forward[level - 1]
        forward.append(value / pivots[level])
    solved = [forward[-1]]
    for level in range(layer_count - 2, -1, -1):
        solved.insert(0, forward[level] - ratios[level] * solved[0])
    stacked = jnp.stack(solved, axis=1)
    return icefield * ((1.0 - RELAX_WEIGHT) * center + RELAX_WEIGHT * stacked)


def reference(velocity, viscosity, friction, ice_mask, obs_tiles, obs_cell, obs_count):
    icefield = jnp.repeat(jnp.repeat(ice_mask.astype(jnp.float32), CX, axis=0), CY, axis=1)
    live_slot = (jnp.arange(CAP, dtype=jnp.int32)[None, None, None, None, :] < obs_count[..., None]).astype(jnp.float32)
    weight = obs_tiles[..., 2, :] * live_slot[..., None]
    owner_x = jnp.arange(BLOCKS_X, dtype=jnp.int32)[None, None, :, None, None]
    owner_y = jnp.arange(BLOCKS_Y, dtype=jnp.int32)[None, None, None, :, None]
    row_global = (owner_x * CX + obs_cell // NB).astype(jnp.int32)
    tile_global = (owner_y * NB + obs_cell % NB).astype(jnp.int32)
    surface = velocity[:, LAYERS - 1].reshape(2, NX, NY // TILE, TILE)
    sampled = surface[:, row_global, tile_global, :]
    observed = jnp.moveaxis(obs_tiles[..., :2, :], -2, 0)
    contrib = weight[None] * (sampled - observed)
    top_layer = jnp.zeros((2, NX, NY // TILE, TILE), jnp.float32).at[:, row_global, tile_global].add(contrib)
    rhs_field = jnp.zeros((2, LAYERS, NX, NY), jnp.float32).at[:, LAYERS - 1].set(top_layer.reshape(2, NX, NY))
    factors = column_factors(jnp.pad(viscosity, ((0, 0), (1, 1), (1, 1))), friction)
    adjoint = jnp.zeros((2, LAYERS, NX, NY), jnp.float32)
    for sweep_index in range(SWEEPS):
        padded = jnp.pad(adjoint, ((0, 0), (0, 0), (1, 1), (1, 1)))
        adjoint = relax(padded, rhs_field, factors, icefield)
    gradient = -icefield * (adjoint[0, 0] * velocity[0, 0] + adjoint[1, 0] * velocity[1, 0])
    return adjoint, gradient
```

```python
import functools

import jax
import jax.numpy as jnp
from jax import lax
from jax.experimental import pallas as pl
from jax.experimental.pallas import tpu as pltpu
from jax.sharding import PartitionSpec as P

MESH = pl.DeviceIdType.MESH
RELAX = 0.8
LANES = 128
HALO = 8
F32 = jnp.float32


def exchange_tiles(nx, ny, tiles, cell, count, got, anchors, row_out, row_in, block, send, recv, own, small_send, small_recv):
    sx, sy = lax.axis_index("gx"), lax.axis_index("gy")
    slots = cell.shape[1]
    me = sx * ny + sy
    barrier = pltpu.get_barrier_semaphore()

    def greet(d, carry):
        ox = lax.rem(sx + d // ny, nx)
        oy = lax.rem(sy + lax.rem(d, ny), ny)
        pl.semaphore_signal(barrier, inc=1, device_id=(ox, oy), device_id_type=MESH)
        return carry

    lax.fori_loop(1, nx * ny, greet, 0)

    row_out[...] = jnp.full(row_out.shape, -1, jnp.int32)
    for oy in range(ny):
        slot = lax.broadcasted_iota(jnp.int32, (slots, nx), 0)
        live = jnp.where(slot < count[oy : oy + 1, :], cell[oy], -1)
        for s in range(slots):
            row_out[oy, :, s * nx : (s + 1) * nx] = live[s : s + 1, :]

    pl.semaphore_wait(barrier, nx * ny - 1)

    def send_row(d):
        oy = lax.rem(sy + d, ny)
        return pltpu.make_async_remote_copy(
            src_ref=row_out.at[oy],
            dst_ref=row_in.at[sy],
            send_sem=small_send.at[0],
            recv_sem=small_recv.at[0],
            device_id=(sx, oy),
            device_id_type=MESH,
        )

    for d in range(1, ny):
        send_row(d).start()
    row_in[pl.ds(sy, 1)] = row_out[pl.ds(sy, 1)]

    mine = pltpu.make_async_copy(tiles.at[me], got.at[me], own)
    mine.start()

    def send_tile(d, carry):
        ox = lax.rem(sx + d // ny, nx)
        oy = lax.rem(sy + lax.rem(d, ny), ny)
        pltpu.make_async_remote_copy(
            src_ref=tiles.at[ox * ny + oy],
            dst_ref=got.at[me],
            send_sem=send,
            recv_sem=recv,
            device_id=(ox, oy),
            device_id_type=MESH,
        ).start()
        return carry

    lax.fori_loop(1, nx * ny // 4, send_tile, 0)

    pltpu.make_async_copy(row_in.at[pl.ds(0, ny - 1)], row_in.at[pl.ds(0, ny - 1)], small_recv.at[0]).wait()
    for y in range(ny):
        block[y : y + 1, :] = row_in[y]

    def send_block(d, carry):
        ox = lax.rem(sx + d, nx)
        pltpu.make_async_remote_copy(
            src_ref=block,
            dst_ref=anchors.at[sx],
            send_sem=small_send.at[1],
            recv_sem=small_recv.at[1],
            device_id=(ox, sy),
            device_id_type=MESH,
        ).start()
        return carry

    lax.fori_loop(1, nx, send_block, 0)
    lax.fori_loop(nx * ny // 4, nx * ny, send_tile, 0)
    anchors[pl.ds(sx, 1)] = block[...].reshape((1,) + block.shape)

    few, many = pl.ds(0, nx - 1), pl.ds(0, nx * ny - 1)
    pltpu.make_async_copy(anchors.at[few], anchors.at[few], small_recv.at[1]).wait()
    pltpu.make_async_copy(got.at[many], got.at[many], recv).wait()
    mine.wait()
    pltpu.make_async_copy(row_in.at[pl.ds(0, ny - 1)], row_in.at[pl.ds(0, ny - 1)], small_send.at[0]).wait()
    pltpu.make_async_copy(anchors.at[few], anchors.at[few], small_send.at[1]).wait()
    pltpu.make_async_copy(got.at[many], got.at[many], send).wait()


def sweeps(nx, ny, tiles, anchors, velocity, viscosity, friction, ice, out, gradient,
           eta, adj_a, adj_b, west, east, south, north, carry_c, ratio_c, top_c, vel, rhs, lookup, total,
           row_s, row_r, col_s, col_r, load_sem, send_sem, recv_sem):
    sx, sy = lax.axis_index("gx"), lax.axis_index("gy")
    layers, nb, rows = west.shape[0], west.shape[1], west.shape[2]
    blocks = rows // 8
    below, above = lax.rem(sx + nx - 1, nx), lax.rem(sx + 1, nx)
    left, right = lax.rem(sy + ny - 1, ny), lax.rem(sy + 1, ny)
    partners = ((below, sy), (above, sy), (sx, left), (sx, right))

    loads = [pltpu.make_async_copy(viscosity.at[:, :, pl.ds(t * LANES, LANES)], eta.at[:, t, pl.ds(HALO, rows), :], load_sem.at[t])
             for t in range(nb)]
    for c in range(2):
        loads.append(pltpu.make_async_copy(velocity.at[c, layers - 1], vel.at[0, c], load_sem.at[nb + 2 * c]))
        loads.append(pltpu.make_async_copy(velocity.at[c, 0], vel.at[1, c], load_sem.at[nb + 2 * c + 1]))
    for load in loads:
        load.start()

    barrier = pltpu.get_barrier_semaphore()
    for partner in partners:
        pl.semaphore_signal(barrier, inc=1, device_id=partner, device_id_type=MESH)
    pl.semaphore_wait(barrier, 4)

    lane = lax.broadcasted_iota(jnp.int32, (8, LANES), 1)
    exists = [jnp.where(e, 1.0, 0.0).astype(F32) for e in (sx > 0, sx < nx - 1, sy > 0, sy < ny - 1)]

    def copies(n):
        made = []
        for side, partner in enumerate(partners):
            src, dst = (row_s, row_r) if side < 2 else (col_s, col_r)
            made.append(pltpu.make_async_remote_copy(
                src_ref=src.at[n, side % 2],
                dst_ref=dst.at[n, 1 - side % 2],
                send_sem=send_sem.at[n, side],
                recv_sem=recv_sem.at[n, side ^ 1],
                device_id=partner,
                device_id_type=MESH,
            ))
        return made

    def pack_rows(n, field, planes):
        for q, plane in enumerate(planes):
            for t in range(nb):
                part = slice(t * LANES, (t + 1) * LANES)
                row_s[n, 0, q : q + 1, part] = field[plane + (t, slice(HALO, HALO + 1))]
                row_s[n, 1, q : q + 1, part] = field[plane + (t, slice(HALO + rows - 1, HALO + rows))]

    def unpack_rows(n, field, planes):
        for q, plane in enumerate(planes):
            for t in range(nb):
                part = slice(t * LANES, (t + 1) * LANES)
                field[plane + (t, slice(HALO - 1, HALO))] = row_r[n, 0, q : q + 1, part] * exists[0]
                field[plane + (t, slice(HALO + rows, HALO + rows + 1))] = row_r[n, 1, q : q + 1, part] * exists[1]

    def at(i, shift=0):
        start = pl.multiple_of(i * 8, 8) + HALO
        return pl.ds(start + shift, 8)

    def sides(tiles_c, left_halo, right_halo):
        ups = [left_halo] + [pltpu.roll(a, 1, 1) for a in tiles_c]
        downs = [pltpu.roll(a, LANES - 1, 1) for a in tiles_c] + [right_halo]
        low = [jnp.where(lane == 0, ups[t], ups[t + 1]) for t in range(nb)]
        high = [jnp.where(lane == LANES - 1, downs[t + 1], downs[t]) for t in range(nb)]
        return low, high

    def halo_cols(n, i, q):
        rows_i = pl.ds(pl.multiple_of(i * 8, 8), 8)
        lo = pltpu.roll(col_r[n, 0, rows_i, :], (LANES - q) % LANES, 1) * exists[2]
        hi = pltpu.roll(col_r[n, 1, rows_i, :], LANES - 1 - q, 1) * exists[3]
        return lo, hi

    def put(packed, q, value, edge):
        return jnp.where(lane == q, pltpu.roll(value, (q - edge) % LANES, 1), packed)

    for t in range(nb):
        loads[t].wait()

    def pack_eta(i, carry):
        low = jnp.zeros((8, LANES), F32)
        high = jnp.zeros((8, LANES), F32)
        for k in range(layers):
            low = put(low, k, eta[k, 0, at(i), :], 0)
            high = put(high, k, eta[k, nb - 1, at(i), :], LANES - 1)
        rows_i = pl.ds(pl.multiple_of(i * 8, 8), 8)
        col_s[0, 0, rows_i, :] = low
        col_s[0, 1, rows_i, :] = high
        return carry

    lax.fori_loop(0, blocks, pack_eta, 0)
    eta_planes = [(k,) for k in range(layers)]
    pack_rows(0, eta, eta_planes)
    eta_copies = copies(0)
    for copy in eta_copies:
        copy.start()

    senders = nx * ny
    slots = tiles.shape[0] // senders // 3
    lookup[...] = jnp.transpose(anchors[...].astype(F32).reshape(senders, LANES))
    spot = lax.broadcasted_iota(jnp.int32, (nb * rows, senders), 0)
    band = jnp.zeros_like(spot)
    for t in range(1, nb):
        band = band + jnp.where(spot >= t * rows, 1, 0)
    spot = ((spot - band * rows) * nb + band).astype(F32)
    for s in range(slots):
        row = lookup[pl.ds(s * nx + sx, 1), :]
        chosen = jnp.where(spot == row, 1.0, 0.0).astype(jnp.bfloat16)
        u, v, w = (tiles[pl.ds(slots * c + s, senders, stride=3 * slots), :] for c in range(3))
        rest = jnp.concatenate([u * w, v * w, w], axis=1)
        for step in range(3):
            part = rest.astype(jnp.bfloat16)
            if step < 2:
                rest = rest - part.astype(F32)
            term = jnp.dot(chosen, part, preferred_element_type=F32)
            if s == 0 and step == 0:
                total[...] = term
            else:
                total[...] += term
    for load in loads[nb:]:
        load.wait()
    for t in range(nb):
        part = slice(t * LANES, (t + 1) * LANES)
        weight = total[t * rows : (t + 1) * rows, 2 * LANES : 3 * LANES]
        for c in range(2):
            rhs[c, t] = weight * vel[0, c, :, part] - total[t * rows : (t + 1) * rows, c * LANES : (c + 1) * LANES]

    for copy in eta_copies:
        copy.wait()
    unpack_rows(0, eta, eta_planes)

    def factor(i, carry):
        rows_i = pl.ds(pl.multiple_of(i * 8, 8), 8)
        last_up = [None] * nb
        last_ratio = [None] * nb
        centre = [eta[0, t, at(i), :] for t in range(nb)]
        for k in range(layers):
            lo_halo, hi_halo = halo_cols(0, i, k)
            low, high = sides(centre, lo_halo, hi_halo)
            upper = [eta[k + 1, t, at(i), :] for t in range(nb)] if k < layers - 1 else None
            for t in range(nb):
                w = 0.5 * (centre[t] + eta[k, t, at(i, -1), :])
                e = 0.5 * (centre[t] + eta[k, t, at(i, 1), :])
                s = 0.5 * (centre[t] + low[t])
                n = 0.5 * (centre[t] + high[t])
                pivot = w + e + s + n
                if k == 0:
                    pivot = pivot + friction[rows_i, t * LANES : (t + 1) * LANES]
                if k < layers - 1:
                    up = centre[t] + upper[t]
                    pivot = pivot + up
                if k > 0:
                    pivot = pivot + last_up[t] - last_up[t] * last_ratio[t]
                inverse = 1.0 / pivot
                west[k, t, rows_i, :] = w * inverse
                east[k, t, rows_i, :] = e * inverse
                south[k, t, rows_i, :] = s * inverse
                north[k, t, rows_i, :] = n * inverse
                if k > 0:
                    carry_c[k - 1, t, rows_i, :] = last_up[t] * inverse
                if k < layers - 1:
                    last_ratio[t] = up * inverse
                    ratio_c[k, t, rows_i, :] = last_ratio[t]
                    last_up[t] = up
                else:
                    top_c[t, rows_i, :] = inverse
            centre = upper
        return carry

    lax.fori_loop(0, blocks, factor, 0)

    icef = ice[0, 0].astype(F32)
    keep, gain = icef * (1.0 - RELAX), icef * RELAX
    planes = [(c, k) for c in range(2) for k in range(layers)]

    def pack_cols(n, i, low, high):
        rows_i = pl.ds(pl.multiple_of(i * 8, 8), 8)
        col_s[n, 0, rows_i, :] = low
        col_s[n, 1, rows_i, :] = high

    def first(i, carry):
        rows_i = pl.ds(pl.multiple_of(i * 8, 8), 8)
        low = jnp.zeros((8, LANES), F32)
        high = jnp.zeros((8, LANES), F32)
        for c in range(2):
            x = []
            for t in range(nb):
                top = rhs[c, t, rows_i, :] * top_c[t, rows_i, :]
                rhs[c, t, rows_i, :] = top
                x.append(gain * top)
            for k in range(layers - 1, -1, -1):
                if k < layers - 1:
                    x = [ratio_c[k, t, rows_i, :] * x[t] for t in range(nb)]
                for t in range(nb):
                    adj_a[c, k, t, at(i), :] = x[t]
                low = put(low, c * layers + k, x[0], 0)
                high = put(high, c * layers + k, x[nb - 1], LANES - 1)
        pack_cols(1, i, low, high)
        return carry

    lax.fori_loop(0, blocks, first, 0)

    def swap(n, field):
        pack_rows(n, field, planes)
        made = copies(n)
        for copy in made:
            copy.start()
        for copy in made:
            copy.wait()
        unpack_rows(n, field, planes)

    def relax(n, i, old, new, last):
        rows_i = pl.ds(pl.multiple_of(i * 8, 8), 8)
        low_p = jnp.zeros((8, LANES), F32)
        high_p = jnp.zeros((8, LANES), F32)
        grad = [None] * nb
        for c in range(2):
            forward = []
            for k in range(layers):
                centre = [old[c, k, t, at(i), :] for t in range(nb)]
                low, high = sides(centre, *halo_cols(n, i, c * layers + k))
                level = []
                for t in range(nb):
                    value = (west[k, t, rows_i, :] * old[c, k, t, at(i, -1), :]
                             + east[k, t, rows_i, :] * old[c, k, t, at(i, 1), :])
                    value = value + (south[k, t, rows_i, :] * low[t] + north[k, t, rows_i, :] * high[t])
                    if k > 0:
                        value = value + carry_c[k - 1, t, rows_i, :] * forward[k - 1][t]
                    if k == layers - 1:
                        value = value + rhs[c, t, rows_i, :]
                    level.append(value)
                forward.append(level)
            x = forward[layers - 1]
            for k in range(layers - 1, -1, -1):
                if k < layers - 1:
                    x = [forward[k][t] + ratio_c[k, t, rows_i, :] * x[t] for t in range(nb)]
                made = [keep * old[c, k, t, at(i), :] + gain * x[t] for t in range(nb)]
                if last:
                    for t in range(nb):
                        out[c, k, rows_i, t * LANES : (t + 1) * LANES] = made[t]
                        if k == 0:
                            term = made[t] * vel[1, c, rows_i, t * LANES : (t + 1) * LANES]
                            grad[t] = term if c == 0 else grad[t] + term
                else:
                    for t in range(nb):
                        new[c, k, t, at(i), :] = made[t]
                    low_p = put(low_p, c * layers + k, made[0], 0)
                    high_p = put(high_p, c * layers + k, made[nb - 1], LANES - 1)
        if last:
            for t in range(nb):
                gradient[rows_i, t * LANES : (t + 1) * LANES] = -icef * grad[t]
        else:
            pack_cols(n + 1, i, low_p, high_p)

    def second(i, carry):
        relax(1, i, adj_a, adj_b, False)
        return carry

    def third(i, carry):
        relax(2, i, adj_b, None, True)
        return carry

    swap(1, adj_a)
    lax.fori_loop(0, blocks, second, 0)
    swap(2, adj_b)
    lax.fori_loop(0, blocks, third, 0)


def per_device(nx, ny, velocity, viscosity, friction, ice_mask, obs_tiles, obs_cell, obs_count):
    comps, layers, rows, cols = velocity.shape
    slots, tile_len = obs_tiles.shape[4], obs_tiles.shape[6]
    nb, senders = cols // tile_len, nx * ny
    in_vmem = pl.BlockSpec(memory_space=pltpu.VMEM)
    in_smem = pl.BlockSpec(memory_space=pltpu.SMEM)
    in_place = pl.BlockSpec(memory_space=pl.ANY)

    tiles = obs_tiles.transpose(0, 1, 2, 3, 5, 4, 6).reshape(senders, 3, slots, tile_len)
    cell = obs_cell.transpose(0, 1, 3, 4, 2).reshape(ny, slots, nx)
    count = obs_count.transpose(0, 1, 3, 2).reshape(ny, nx)
    got, anchors = pl.pallas_call(
        functools.partial(exchange_tiles, nx, ny),
        out_shape=(
            jax.ShapeDtypeStruct((senders, 3, slots, tile_len), F32),
            jax.ShapeDtypeStruct((nx, ny, LANES), jnp.int32),
        ),
        in_specs=[in_place, in_vmem, in_vmem],
        out_specs=(in_place, in_vmem),
        scratch_shapes=[
            pltpu.VMEM((ny, 1, LANES), jnp.int32),
            pltpu.VMEM((ny, 1, LANES), jnp.int32),
            pltpu.VMEM((ny, LANES), jnp.int32),
            pltpu.SemaphoreType.DMA,
            pltpu.SemaphoreType.DMA,
            pltpu.SemaphoreType.DMA,
            pltpu.SemaphoreType.DMA((2,)),
            pltpu.SemaphoreType.DMA((2,)),
        ],
        compiler_params=pltpu.CompilerParams(collective_id=0, has_side_effects=True),
        name="tile_exchange",
    )(tiles, cell, count)

    halo_rows = rows + 2 * HALO
    packed = -(-comps * layers // 8) * 8
    face = pltpu.VMEM((layers, nb, rows, LANES), F32)
    link = pltpu.VMEM((layers - 1, nb, rows, LANES), F32)
    field = pltpu.VMEM((comps, layers, nb, halo_rows, LANES), F32)
    return pl.pallas_call(
        functools.partial(sweeps, nx, ny),
        out_shape=(
            jax.ShapeDtypeStruct(velocity.shape, F32),
            jax.ShapeDtypeStruct((rows, cols), F32),
        ),
        in_specs=[in_vmem, in_vmem, in_place, in_place, in_vmem, in_smem],
        out_specs=(in_vmem, in_vmem),
        scratch_shapes=[
            pltpu.VMEM((layers, nb, halo_rows, LANES), F32),
            field,
            field,
            face,
            face,
            face,
            face,
            link,
            link,
            pltpu.VMEM((nb, rows, LANES), F32),
            pltpu.VMEM((2, comps, rows, cols), F32),
            pltpu.VMEM((comps, nb, rows, LANES), F32),
            pltpu.VMEM((LANES, senders), F32),
            pltpu.VMEM((nb * rows, 3 * LANES), F32),
            pltpu.VMEM((3, 2, packed, cols), F32),
            pltpu.VMEM((3, 2, packed, cols), F32),
            pltpu.VMEM((3, 2, rows, LANES), F32),
            pltpu.VMEM((3, 2, rows, LANES), F32),
            pltpu.SemaphoreType.DMA((nb + 4,)),
            pltpu.SemaphoreType.DMA((3, 4)),
            pltpu.SemaphoreType.DMA((3, 4)),
        ],
        compiler_params=pltpu.CompilerParams(
            collective_id=1, has_side_effects=True, vmem_limit_bytes=56 * 2**20
        ),
        name="line_sweeps",
    )(got.reshape(senders * 3 * slots, tile_len), anchors, velocity, viscosity, friction, ice_mask)


def solution(mesh):
    placed = (
        P(None, None, "gx", "gy"),
        P(None, "gx", "gy"),
        P("gx", "gy"),
        P("gx", "gy"),
        P("gx", "gy", None, None, None, None, None),
        P("gx", "gy", None, None, None),
        P("gx", "gy", None, None),
    )
    return jax.shard_map(
        functools.partial(per_device, mesh.shape["gx"], mesh.shape["gy"]),
        mesh=mesh,
        in_specs=placed,
        out_specs=(P(None, None, "gx", "gy"), P("gx", "gy")),
        check_vma=False,
    )
```

```python
import functools

import jax
import jax.numpy as jnp
from jax import lax
from jax.experimental import pallas as pl
from jax.experimental.pallas import tpu as pltpu
from jax.sharding import PartitionSpec as P

MESH = pl.DeviceIdType.MESH
RELAX = 0.8
LANES = 128
HALO = 8
F32 = jnp.float32


def shifts(nb, lane, values, low_halo, high_halo):
    ups = [low_halo] + [pltpu.roll(a, 1, 1) for a in values]
    downs = [pltpu.roll(a, LANES - 1, 1) for a in values] + [high_halo]
    low = [jnp.where(lane == 0, ups[t], ups[t + 1]) for t in range(nb)]
    high = [jnp.where(lane == LANES - 1, downs[t + 1], downs[t]) for t in range(nb)]
    return low, high


def at(i, shift=0):
    return pl.ds(pl.multiple_of(i * 8, 8) + HALO + shift, 8)


def plain(i):
    return pl.ds(pl.multiple_of(i * 8, 8), 8)


def halo_cols(packed, i, q, exists):
    lo = pltpu.roll(packed[0, plain(i), :], (LANES - q) % LANES, 1) * exists[0]
    hi = pltpu.roll(packed[1, plain(i), :], LANES - 1 - q, 1) * exists[1]
    return lo, hi


def put(packed, lane, q, value, edge):
    return jnp.where(lane == q, pltpu.roll(value, (q - edge) % LANES, 1), packed)


def solve(i, c, lane, nb, old, cols, exists, faces, carry_c, ratio_c, rhs, keep, gain, emit):
    west, east, south, north = faces
    layers, r = west.shape[0], plain(i)
    forward = []
    for k in range(layers):
        centre = [old[c, k, t, at(i), :] for t in range(nb)]
        low, high = shifts(nb, lane, centre, *halo_cols(cols, i, c * layers + k, exists))
        level = []
        for t in range(nb):
            value = west[k, t, r, :] * old[c, k, t, at(i, -1), :] + east[k, t, r, :] * old[c, k, t, at(i, 1), :]
            value = value + (south[k, t, r, :] * low[t] + north[k, t, r, :] * high[t])
            if k > 0:
                value = value + carry_c[k - 1, t, r, :] * forward[k - 1][t]
            if k == layers - 1:
                value = value + rhs[c, t, r, :]
            level.append(value)
        forward.append(level)
    x = forward[layers - 1]
    for k in range(layers - 1, -1, -1):
        if k < layers - 1:
            x = [forward[k][t] + ratio_c[k, t, r, :] * x[t] for t in range(nb)]
        emit(k, [keep * old[c, k, t, at(i), :] + gain * x[t] for t in range(nb)])


def gather_and_sweep(nx, ny, width, staged, tiles, cell, count, velocity, viscosity, friction, ice,
                     adj_b, west, east, south, north, carry_c, ratio_c, rhs, cols_b,
                     eta, adj_a, top_c, vel, fric, cell_v, count_v, mid, got, row_out, row_in, block, anchors, lookup, total,
                     row_s, row_r, col_s, col_r,
                     load_sem, send_sem, recv_sem, entered, z_send, z_recv, own, far_send, far_recv, near_send, near_recv,
                     small_send, small_recv):
    sx, sy = lax.axis_index("gx"), lax.axis_index("gy")
    layers, nb, rows = west.shape[0], west.shape[1], west.shape[2]
    slots, groups, blocks = cell_v.shape[1], nx // width, rows // 8

    def x_at(d):
        return lax.rem(sx + d, nx)

    def y_at(d):
        return lax.rem(sy + d, ny)

    barrier = pltpu.get_barrier_semaphore()
    for d in range(1, ny):
        pl.semaphore_signal(barrier, inc=1, device_id=(sx, y_at(d)), device_id_type=MESH)

    def greet(d, carry):
        pl.semaphore_signal(barrier, inc=1, device_id=(x_at(d), sy), device_id_type=MESH)
        return carry

    lax.fori_loop(1, nx, greet, 0)

    loads = [pltpu.make_async_copy(cell, cell_v, load_sem.at[0]), pltpu.make_async_copy(count, count_v, load_sem.at[1])]
    for t in range(nb):
        part = pl.ds(t * LANES, LANES)
        loads.append(pltpu.make_async_copy(viscosity.at[:, :, part], eta.at[:, t, pl.ds(HALO, rows), :], load_sem.at[2 + t]))
    loads.append(pltpu.make_async_copy(friction, fric, load_sem.at[2 + nb]))
    for c in range(2):
        loads.append(pltpu.make_async_copy(velocity.at[c, layers - 1], vel.at[c], load_sem.at[3 + nb + c]))
    kept = pltpu.make_async_copy(tiles.at[:, sy], mid.at[:, sy], own.at[0])
    for load in loads:
        load.start()
    kept.start()

    row_out[...] = jnp.full(row_out.shape, -1, jnp.int32)
    for load in loads[:2]:
        load.wait()
    for oy in range(ny):
        slot = lax.broadcasted_iota(jnp.int32, (slots, nx), 0)
        live = jnp.where(slot < count_v[oy : oy + 1, :], cell_v[oy], -1)
        for s in range(slots):
            row_out[oy, :, s * nx : (s + 1) * nx] = live[s : s + 1, :]

    pl.semaphore_wait(barrier, nx + ny - 2)

    for d in range(1, ny):
        pl.semaphore_signal(entered, inc=1, device_id=(sx, y_at(d)), device_id_type=MESH)

    def group(g):
        return lax.rem(sx // width + g, groups) * width

    def remote(src, dst, send, recv, ox, oy):
        return pltpu.make_async_remote_copy(
            src_ref=src, dst_ref=dst, send_sem=send, recv_sem=recv, device_id=(ox, oy), device_id_type=MESH
        )

    for d in range(1, ny):
        remote(row_out.at[y_at(d)], row_in.at[sy], small_send.at[0], small_recv.at[0], sx, y_at(d)).start()
    for g in range(staged):
        some = pl.ds(group(g), width)
        for d in range(1, ny):
            remote(tiles.at[some, y_at(d)], mid.at[some, sy], z_send.at[g], z_recv.at[g], sx, y_at(d)).start()
    row_in[pl.ds(sy, 1)] = row_out[pl.ds(sy, 1)]

    partners = ((x_at(nx - 1), sy), (x_at(1), sy), (sx, y_at(ny - 1)), (sx, y_at(1)))
    lane = lax.broadcasted_iota(jnp.int32, (8, LANES), 1)
    exists = [jnp.where(e, 1.0, 0.0).astype(F32) for e in (sx > 0, sx < nx - 1, sy > 0, sy < ny - 1)]

    def swap(n, field, planes):
        for q, plane in enumerate(planes):
            for t in range(nb):
                part = slice(t * LANES, (t + 1) * LANES)
                row_s[n, 0, q : q + 1, part] = field[plane + (t, slice(HALO, HALO + 1))]
                row_s[n, 1, q : q + 1, part] = field[plane + (t, slice(HALO + rows - 1, HALO + rows))]
        made = []
        for side, (ox, oy) in enumerate(partners):
            src = (row_s if side < 2 else col_s).at[n, side % 2]
            if side < 2:
                dst = row_r.at[n, 1 - side % 2]
            else:
                dst = cols_b.at[1 - side % 2] if n == 2 else col_r.at[n, 1 - side % 2]
            made.append(remote(src, dst, send_sem.at[n, side], recv_sem.at[n, side ^ 1], ox, oy))
        for copy in made:
            copy.start()

        def finish():
            for copy in made:
                copy.wait()
            for q, plane in enumerate(planes):
                for t in range(nb):
                    part = slice(t * LANES, (t + 1) * LANES)
                    field[plane + (t, slice(HALO - 1, HALO))] = row_r[n, 0, q : q + 1, part] * exists[0]
                    field[plane + (t, slice(HALO + rows, HALO + rows + 1))] = row_r[n, 1, q : q + 1, part] * exists[1]

        return finish

    pl.semaphore_wait(entered, ny - 1)

    def send_group(g):
        def send_tile(d, carry):
            ox = group(g) + lax.rem(sx + d // ny, width)
            oy = y_at(lax.rem(d, ny))
            remote(tiles.at[ox, oy], got.at[sx, sy], far_send, far_recv, ox, oy).start()
            return carry

        lax.fori_loop(0, width * ny, send_tile, 0)

    third = (groups - staged) // 3
    for g in range(staged, staged + third):
        send_group(g)

    for t in range(nb):
        loads[2 + t].wait()

    def pack_eta(i, carry):
        low = jnp.zeros((8, LANES), F32)
        high = jnp.zeros((8, LANES), F32)
        for k in range(layers):
            low = put(low, lane, k, eta[k, 0, at(i), :], 0)
            high = put(high, lane, k, eta[k, nb - 1, at(i), :], LANES - 1)
        col_s[0, 0, plain(i), :] = low
        col_s[0, 1, plain(i), :] = high
        return carry

    lax.fori_loop(0, blocks, pack_eta, 0)
    finish_eta = swap(0, eta, [(k,) for k in range(layers)])

    arrived = row_in.at[pl.ds(0, ny - 1)]
    pltpu.make_async_copy(arrived, arrived, small_recv.at[0]).wait()
    for y in range(ny):
        block[y : y + 1, :] = row_in[y]

    def send_block(d, carry):
        remote(block, anchors.at[sx], small_send.at[1], small_recv.at[1], x_at(d), sy).start()
        return carry

    lax.fori_loop(1, nx, send_block, 0)
    anchors[pl.ds(sx, 1)] = block[...].reshape((1,) + block.shape)

    kept.wait()
    for g in range(staged):
        if g > 0:
            for more in range(staged + third * g, groups if g == staged - 1 else staged + third * (g + 1)):
                send_group(more)
        bunch = mid.at[pl.ds(0, width), pl.ds(0, ny - 1)]
        pltpu.make_async_copy(bunch, bunch, z_recv.at[g]).wait()
        for j in range(width):
            ox = group(g) + lax.rem(sx + j, width)
            if g == 0 and j == 0:
                pltpu.make_async_copy(mid.at[sx], got.at[sx], own.at[1]).start()
            else:
                remote(mid.at[ox], got.at[sx], near_send, near_recv, ox, sy).start()

    finish_eta()
    loads[2 + nb].wait()

    def factor(i, carry):
        r = plain(i)
        last_up = [None] * nb
        last_ratio = [None] * nb
        centre = [eta[0, t, at(i), :] for t in range(nb)]
        for k in range(layers):
            low, high = shifts(nb, lane, centre, *halo_cols(col_r.at[0], i, k, exists[2:]))
            upper = [eta[k + 1, t, at(i), :] for t in range(nb)] if k < layers - 1 else None
            for t in range(nb):
                w = 0.5 * (centre[t] + eta[k, t, at(i, -1), :])
                e = 0.5 * (centre[t] + eta[k, t, at(i, 1), :])
                s = 0.5 * (centre[t] + low[t])
                n = 0.5 * (centre[t] + high[t])
                pivot = w + e + s + n
                if k == 0:
                    pivot = pivot + fric[r, t * LANES : (t + 1) * LANES]
                if k < layers - 1:
                    up = centre[t] + upper[t]
                    pivot = pivot + up
                if k > 0:
                    pivot = pivot + last_up[t] - last_up[t] * last_ratio[t]
                inverse = 1.0 / pivot
                west[k, t, r, :] = w * inverse
                east[k, t, r, :] = e * inverse
                south[k, t, r, :] = s * inverse
                north[k, t, r, :] = n * inverse
                if k > 0:
                    carry_c[k - 1, t, r, :] = last_up[t] * inverse
                if k < layers - 1:
                    last_ratio[t] = up * inverse
                    ratio_c[k, t, r, :] = last_ratio[t]
                    last_up[t] = up
                else:
                    top_c[t, r, :] = inverse
            centre = upper
        return carry

    lax.fori_loop(0, blocks, factor, 0)

    few = anchors.at[pl.ds(0, nx - 1)]
    pltpu.make_async_copy(few, few, small_recv.at[1]).wait()
    senders = nx * ny
    lookup[...] = jnp.transpose(anchors[...].astype(F32).reshape(senders, LANES))
    spot = lax.broadcasted_iota(jnp.int32, (nb * rows, senders), 0)
    band = jnp.zeros_like(spot)
    for t in range(1, nb):
        band = band + jnp.where(spot >= t * rows, 1, 0)
    spot = ((spot - band * rows) * nb + band).astype(F32)
    for load in loads[3 + nb :]:
        load.wait()
    far = got.at[pl.ds(0, (groups - staged) * width)]
    pltpu.make_async_copy(far, far, far_recv).wait()
    near = got.at[pl.ds(0, staged * width - 1)]
    pltpu.make_async_copy(near, near, near_recv).wait()
    pltpu.make_async_copy(mid.at[sx], got.at[sx], own.at[1]).wait()
    flat = got.reshape(senders * 3 * slots, LANES)
    for s in range(slots):
        row = lookup[pl.ds(s * nx + sx, 1), :]
        chosen = jnp.where(spot == row, 1.0, 0.0).astype(jnp.bfloat16)
        u, v, w = (flat[pl.ds(slots * c + s, senders, stride=3 * slots), :] for c in range(3))
        rest = jnp.concatenate([u * w, v * w, w], axis=1)
        for step in range(3):
            part = rest.astype(jnp.bfloat16)
            if step < 2:
                rest = rest - part.astype(F32)
            term = jnp.dot(chosen, part, preferred_element_type=F32)
            if s == 0 and step == 0:
                total[...] = term
            else:
                total[...] += term
    for t in range(nb):
        part = slice(t * LANES, (t + 1) * LANES)
        weight = total[t * rows : (t + 1) * rows, 2 * LANES : 3 * LANES]
        for c in range(2):
            rhs[c, t] = weight * vel[c, :, part] - total[t * rows : (t + 1) * rows, c * LANES : (c + 1) * LANES]

    icef = ice[0, 0].astype(F32)
    keep, gain = icef * (1.0 - RELAX), icef * RELAX
    planes = [(c, k) for c in range(2) for k in range(layers)]

    def first(i, carry):
        r = plain(i)
        low = jnp.zeros((8, LANES), F32)
        high = jnp.zeros((8, LANES), F32)
        for c in range(2):
            x = []
            for t in range(nb):
                top = rhs[c, t, r, :] * top_c[t, r, :]
                rhs[c, t, r, :] = top
                x.append(gain * top)
            for k in range(layers - 1, -1, -1):
                if k < layers - 1:
                    x = [ratio_c[k, t, r, :] * x[t] for t in range(nb)]
                for t in range(nb):
                    adj_a[c, k, t, at(i), :] = x[t]
                low = put(low, lane, c * layers + k, x[0], 0)
                high = put(high, lane, c * layers + k, x[nb - 1], LANES - 1)
        col_s[1, 0, r, :] = low
        col_s[1, 1, r, :] = high
        return carry

    lax.fori_loop(0, blocks, first, 0)
    swap(1, adj_a, planes)()

    def second(i, carry):
        edges = [jnp.zeros((8, LANES), F32), jnp.zeros((8, LANES), F32)]
        for c in range(2):
            def emit(k, made):
                for t in range(nb):
                    adj_b[c, k, t, at(i), :] = made[t]
                edges[0] = put(edges[0], lane, c * layers + k, made[0], 0)
                edges[1] = put(edges[1], lane, c * layers + k, made[nb - 1], LANES - 1)

            solve(i, c, lane, nb, adj_a, col_r.at[1], exists[2:], (west, east, south, north), carry_c, ratio_c, rhs, keep, gain, emit)
        col_s[2, 0, plain(i), :] = edges[0]
        col_s[2, 1, plain(i), :] = edges[1]
        return carry

    lax.fori_loop(0, blocks, second, 0)
    finish_b = swap(2, adj_b, planes)

    pltpu.make_async_copy(arrived, arrived, small_send.at[0]).wait()
    pltpu.make_async_copy(few, few, small_send.at[1]).wait()
    for g in range(staged):
        bunch = mid.at[pl.ds(0, width), pl.ds(0, ny - 1)]
        pltpu.make_async_copy(bunch, bunch, z_send.at[g]).wait()
    pltpu.make_async_copy(far, far, far_send).wait()
    pltpu.make_async_copy(near, near, near_send).wait()
    finish_b()


def last_sweep(pieces, ny, adj_b, west, east, south, north, carry_c, ratio_c, rhs, cols_b, velocity, ice,
               out, gradient, made_v, grad_v, vel, load_sem, store_sem):
    sy = lax.axis_index("gy")
    layers, nb, rows = west.shape[0], west.shape[1], west.shape[2]
    loads = [pltpu.make_async_copy(velocity.at[c, 0], vel.at[c], load_sem.at[c]) for c in range(2)]
    for load in loads:
        load.start()
    lane = lax.broadcasted_iota(jnp.int32, (8, LANES), 1)
    exists = [jnp.where(e, 1.0, 0.0).astype(F32) for e in (sy > 0, sy < ny - 1)]
    icef = ice[0, 0].astype(F32)
    keep, gain = icef * (1.0 - RELAX), icef * RELAX
    for load in loads:
        load.wait()

    def third(i, carry):
        r = plain(i)
        grad = [None] * nb
        for c in range(2):
            def emit(k, made):
                for t in range(nb):
                    part = slice(t * LANES, (t + 1) * LANES)
                    made_v[c, k, r, part] = made[t]
                    if k == 0:
                        term = made[t] * vel[c, r, part]
                        grad[t] = term if c == 0 else grad[t] + term

            solve(i, c, lane, nb, adj_b, cols_b, exists, (west, east, south, north), carry_c, ratio_c, rhs, keep, gain, emit)
        for t in range(nb):
            grad_v[r, t * LANES : (t + 1) * LANES] = -icef * grad[t]
        return carry

    blocks = rows // 8
    each = -(-blocks // pieces)
    stores = []
    for p in range(0, blocks, each):
        stop = min(p + each, blocks)
        lax.fori_loop(p, stop, third, 0)
        some = pl.ds(p * 8, (stop - p) * 8)
        stores.append(pltpu.make_async_copy(made_v.at[:, :, some, :], out.at[:, :, some, :], store_sem.at[len(stores)]))
        stores[-1].start()
    stores.append(pltpu.make_async_copy(grad_v, gradient, store_sem.at[len(stores)]))
    stores[-1].start()
    for store in stores:
        store.wait()


def per_device(nx, ny, velocity, viscosity, friction, ice_mask, obs_tiles, obs_cell, obs_count):
    comps, layers, rows, cols = velocity.shape
    slots, tile_len = obs_tiles.shape[4], obs_tiles.shape[6]
    nb = cols // tile_len
    width = max(1, nx // 8)
    staged, pieces = 2, 4
    in_vmem = pl.BlockSpec(memory_space=pltpu.VMEM)
    in_smem = pl.BlockSpec(memory_space=pltpu.SMEM)
    in_place = pl.BlockSpec(memory_space=pltpu.HBM)
    dma = pltpu.SemaphoreType.DMA

    tiles = obs_tiles.transpose(0, 1, 2, 3, 5, 4, 6).reshape(nx, ny, 3, slots, tile_len)
    cell = obs_cell.transpose(0, 1, 3, 4, 2).reshape(ny, slots, nx)
    count = obs_count.transpose(0, 1, 3, 2).reshape(ny, nx)
    halo_rows = rows + 2 * HALO
    packed = -(-comps * layers // 8) * 8
    face = pltpu.VMEM((layers, nb, rows, LANES), F32)
    link = pltpu.VMEM((layers - 1, nb, rows, LANES), F32)
    field = pltpu.VMEM((comps, layers, nb, halo_rows, LANES), F32)
    everyone = pltpu.VMEM((nx, ny, 3, slots, tile_len), F32)
    tiles, cell, count, velocity, viscosity, friction = (
        pltpu.with_memory_space_constraint(a, pltpu.HBM) for a in (tiles, cell, count, velocity, viscosity, friction)
    )
    state = pl.pallas_call(
        functools.partial(gather_and_sweep, nx, ny, width, staged),
        out_shape=(
            field, face, face, face, face, link, link,
            pltpu.VMEM((comps, nb, rows, LANES), F32),
            pltpu.VMEM((2, rows, LANES), F32),
        ),
        in_specs=[in_place] * 6 + [in_smem],
        out_specs=(in_vmem,) * 9,
        scratch_shapes=[
            pltpu.VMEM((layers, nb, halo_rows, LANES), F32),
            field,
            pltpu.VMEM((nb, rows, LANES), F32),
            pltpu.VMEM((comps, rows, cols), F32),
            pltpu.VMEM((rows, cols), F32),
            pltpu.VMEM((ny, slots, nx), jnp.int32),
            pltpu.VMEM((ny, nx), jnp.int32),
            everyone,
            everyone,
            pltpu.VMEM((ny, 1, LANES), jnp.int32),
            pltpu.VMEM((ny, 1, LANES), jnp.int32),
            pltpu.VMEM((ny, LANES), jnp.int32),
            pltpu.VMEM((nx, ny, LANES), jnp.int32),
            pltpu.VMEM((LANES, nx * ny), F32),
            pltpu.VMEM((nb * rows, 3 * LANES), F32),
            pltpu.VMEM((3, 2, packed, cols), F32),
            pltpu.VMEM((3, 2, packed, cols), F32),
            pltpu.VMEM((3, 2, rows, LANES), F32),
            pltpu.VMEM((2, 2, rows, LANES), F32),
            dma((nb + 5,)),
            dma((3, 4)),
            dma((3, 4)),
            pltpu.SemaphoreType.REGULAR,
            dma((staged,)),
            dma((staged,)),
            dma((2,)),
            dma, dma, dma, dma,
            dma((2,)),
            dma((2,)),
        ],
        compiler_params=pltpu.CompilerParams(collective_id=0, has_side_effects=True, vmem_limit_bytes=24 * 2**20),
        name="gather_and_sweep",
    )(tiles, cell, count, velocity, viscosity, friction, ice_mask)
    state = [pltpu.with_memory_space_constraint(a, pltpu.VMEM) for a in state]
    return pl.pallas_call(
        functools.partial(last_sweep, pieces, ny),
        out_shape=(
            jax.ShapeDtypeStruct(velocity.shape, F32),
            jax.ShapeDtypeStruct((rows, cols), F32),
        ),
        in_specs=[in_vmem] * 9 + [in_place, in_smem],
        out_specs=(in_place, in_place),
        scratch_shapes=[
            pltpu.VMEM((comps, layers, rows, cols), F32),
            pltpu.VMEM((rows, cols), F32),
            pltpu.VMEM((comps, rows, cols), F32),
            dma((2,)),
            dma((pieces + 1,)),
        ],
        compiler_params=pltpu.CompilerParams(vmem_limit_bytes=16 * 2**20),
        name="last_sweep",
    )(*state, velocity, ice_mask)


def solution(mesh):
    placed = (
        P(None, None, "gx", "gy"),
        P(None, "gx", "gy"),
        P("gx", "gy"),
        P("gx", "gy"),
        P("gx", "gy", None, None, None, None, None),
        P("gx", "gy", None, None, None),
        P("gx", "gy", None, None),
    )
    return jax.shard_map(
        functools.partial(per_device, mesh.shape["gx"], mesh.shape["gy"]),
        mesh=mesh,
        in_specs=placed,
        out_specs=(P(None, None, "gx", "gy"), P("gx", "gy")),
        check_vma=False,
    )
```

```python
import functools

import jax
import jax.numpy as jnp
from jax import lax
from jax.experimental import pallas as pl
from jax.experimental.pallas import tpu as pltpu
from jax.sharding import PartitionSpec as P

MESH = pl.DeviceIdType.MESH
RELAX = 0.8
LANES = 128
HALO = 8
F32 = jnp.float32


def beside(lane, value, before, after):
    low = pltpu.roll(jnp.where(lane == LANES - 1, before, value), 1, 1)
    high = pltpu.roll(jnp.where(lane == 0, after, value), LANES - 1, 1)
    return low, high


def at(i, shift=0):
    return pl.ds(pl.multiple_of(i * 8, 8) + HALO + shift, 8)


def plain(i):
    return pl.ds(pl.multiple_of(i * 8, 8), 8)


def edge_tile(packed, side, i, q):
    return pltpu.roll(packed[side, plain(i), :], (LANES - 1 - q if side == 0 else LANES - q) % LANES, 1)


def put(packed, lane, q, value, edge):
    return jnp.where(lane == q, pltpu.roll(value, (q - edge) % LANES, 1), packed)


def solve(i, t, lane, nb, old, cols, faces, carry_c, ratio_c, rhs, keep, gain, emit):
    west, east, south, north = faces
    layers, r, both = west.shape[0], plain(i), range(2)
    centre, forward = [], []
    for k in range(layers):
        w, e, s, n = (face[k, t, r, :] for face in faces)
        link = carry_c[k - 1, t, r, :] if k > 0 else None
        here, level = [], []
        for c in both:
            a = old[c, k, t, at(i), :]
            q = c * layers + k
            before = old[c, k, t - 1, at(i), :] if t > 0 else edge_tile(cols, 0, i, q)
            after = old[c, k, t + 1, at(i), :] if t < nb - 1 else edge_tile(cols, 1, i, q)
            low, high = beside(lane, a, before, after)
            value = (w * old[c, k, t, at(i, -1), :] + e * old[c, k, t, at(i, 1), :]) + (s * low + n * high)
            if k > 0:
                value = value + link * forward[k - 1][c]
            if k == layers - 1:
                value = value + rhs[c, t, r, :]
            here.append(a)
            level.append(value)
        centre.append(here)
        forward.append(level)
    x = forward[layers - 1]
    for k in range(layers - 1, -1, -1):
        if k < layers - 1:
            ratio = ratio_c[k, t, r, :]
            x = [forward[k][c] + ratio * x[c] for c in both]
        for c in both:
            emit(c, k, keep * centre[k][c] + gain * x[c])


def gather_and_sweep(nx, ny, width, staged, tiles, cell, count, velocity, viscosity, friction, ice,
                     adj_b, west, east, south, north, carry_c, ratio_c, rhs, cols_b,
                     eta, adj_a, coef, top_c, vel, fric, cell_v, count_v, mid, got, row_out, row_in, block, anchors, lookup, total,
                     row_s, row_r, col_s, col_r,
                     load_sem, send_sem, recv_sem, entered, z_send, z_recv, own, far_send, far_recv, near_send, near_recv,
                     small_send, small_recv):
    sx, sy = lax.axis_index("gx"), lax.axis_index("gy")
    layers, nb, rows = west.shape[0], west.shape[1], west.shape[2]
    slots, groups, blocks = cell_v.shape[1], nx // width, rows // 8

    def x_at(d):
        return lax.rem(sx + d, nx)

    def y_at(d):
        return lax.rem(sy + d, ny)

    barrier = pltpu.get_barrier_semaphore()
    for d in range(1, ny):
        pl.semaphore_signal(barrier, inc=1, device_id=(sx, y_at(d)), device_id_type=MESH)

    def greet(d, carry):
        pl.semaphore_signal(barrier, inc=1, device_id=(x_at(d), sy), device_id_type=MESH)
        return carry

    lax.fori_loop(1, nx, greet, 0)

    loads = [pltpu.make_async_copy(cell, cell_v, load_sem.at[0]), pltpu.make_async_copy(count, count_v, load_sem.at[1])]
    for t in range(nb):
        part = pl.ds(t * LANES, LANES)
        loads.append(pltpu.make_async_copy(viscosity.at[:, :, part], eta.at[:, t, pl.ds(HALO, rows), :], load_sem.at[2 + t]))
    loads.append(pltpu.make_async_copy(friction, fric, load_sem.at[2 + nb]))
    for c in range(2):
        loads.append(pltpu.make_async_copy(velocity.at[c, layers - 1], vel.at[c], load_sem.at[3 + nb + c]))
    kept = pltpu.make_async_copy(tiles.at[:, sy], mid.at[:, sy], own.at[0])
    for load in loads:
        load.start()
    kept.start()

    row_out[...] = jnp.full(row_out.shape, -1, jnp.int32)
    for load in loads[:2]:
        load.wait()
    for oy in range(ny):
        slot = lax.broadcasted_iota(jnp.int32, (slots, nx), 0)
        live = jnp.where(slot < count_v[oy : oy + 1, :], cell_v[oy], -1)
        for s in range(slots):
            row_out[oy, :, s * nx : (s + 1) * nx] = live[s : s + 1, :]

    pl.semaphore_wait(barrier, nx + ny - 2)

    for d in range(1, ny):
        pl.semaphore_signal(entered, inc=1, device_id=(sx, y_at(d)), device_id_type=MESH)

    def group(g):
        return lax.rem(sx // width + g, groups) * width

    def remote(src, dst, send, recv, ox, oy):
        return pltpu.make_async_remote_copy(
            src_ref=src, dst_ref=dst, send_sem=send, recv_sem=recv, device_id=(ox, oy), device_id_type=MESH
        )

    for d in range(1, ny):
        remote(row_out.at[y_at(d)], row_in.at[sy], small_send.at[0], small_recv.at[0], sx, y_at(d)).start()
    for g in range(staged):
        some = pl.ds(group(g), width)
        for d in range(1, ny):
            remote(tiles.at[some, y_at(d)], mid.at[some, sy], z_send.at[g], z_recv.at[g], sx, y_at(d)).start()
    row_in[pl.ds(sy, 1)] = row_out[pl.ds(sy, 1)]

    partners = ((x_at(nx - 1), sy), (x_at(1), sy), (sx, y_at(ny - 1)), (sx, y_at(1)))
    lane = lax.broadcasted_iota(jnp.int32, (8, LANES), 1)
    exists = [jnp.where(e, 1.0, 0.0).astype(F32) for e in (sx > 0, sx < nx - 1, sy > 0, sy < ny - 1)]

    def swap(n, take):
        count_q = len(take)
        for q, rows_of in enumerate(take):
            for t in range(nb):
                part = slice(t * LANES, (t + 1) * LANES)
                row_s[n, 0, q : q + 1, part] = rows_of(t, 0)
                row_s[n, 1, q : q + 1, part] = rows_of(t, rows - 1)
        some = pl.ds(0, -(-count_q // 8) * 8)
        made = []
        for side, (ox, oy) in enumerate(partners):
            if side < 2:
                src, dst = row_s.at[n, side % 2, some], row_r.at[n, 1 - side % 2, some]
            else:
                src, dst = col_s.at[n, side % 2], (cols_b.at[1 - side % 2] if n == 3 else col_r.at[n, 1 - side % 2])
            made.append(remote(src, dst, send_sem.at[n, side], recv_sem.at[n, side ^ 1], ox, oy))
        for copy in made:
            copy.start()

        def finish():
            for copy in made:
                copy.wait()
            for side in range(2):
                if n == 3:
                    cols_b[side] = cols_b[side] * exists[2 + side]
                else:
                    col_r[n, side] = col_r[n, side] * exists[2 + side]
                row_r[n, side, some] = row_r[n, side, some] * exists[side]

        return finish

    def rows_in(field, plane):
        return lambda t, r: field[plane + (t, slice(HALO + r, HALO + r + 1))]

    def fill_rows(field, plane, values):
        for side, r in ((0, HALO - 1), (1, HALO + rows)):
            for t in range(nb):
                field[plane + (t, slice(r, r + 1))] = values[side][:, t * LANES : (t + 1) * LANES]

    def pack_cols(n, planes, tile_at):
        def pack(i, carry):
            low = jnp.zeros((8, LANES), F32)
            high = jnp.zeros((8, LANES), F32)
            for q, plane in enumerate(planes):
                low = put(low, lane, q, tile_at(plane, 0, i), 0)
                high = put(high, lane, q, tile_at(plane, nb - 1, i), LANES - 1)
            col_s[n, 0, plain(i), :] = low
            col_s[n, 1, plain(i), :] = high
            return carry

        lax.fori_loop(0, blocks, pack, 0)

    pl.semaphore_wait(entered, ny - 1)

    def send_group(g):
        def send_tile(d, carry):
            ox = group(g) + lax.rem(sx + d // ny, width)
            oy = y_at(lax.rem(d, ny))
            remote(tiles.at[ox, oy], got.at[sx, sy], far_send, far_recv, ox, oy).start()
            return carry

        lax.fori_loop(0, width * ny, send_tile, 0)

    third = (groups - staged) // 3
    for g in range(staged, staged + third):
        send_group(g)

    for t in range(nb):
        loads[2 + t].wait()

    single = [(k,) for k in range(layers)]
    pack_cols(0, single, lambda plane, t, i: eta[plane + (t, at(i))])
    finish_eta = swap(0, [rows_in(eta, plane) for plane in single])

    arrived = row_in.at[pl.ds(0, ny - 1)]
    pltpu.make_async_copy(arrived, arrived, small_recv.at[0]).wait()
    for y in range(ny):
        block[y : y + 1, :] = row_in[y]

    def send_block(d, carry):
        remote(block, anchors.at[sx], small_send.at[1], small_recv.at[1], x_at(d), sy).start()
        return carry

    lax.fori_loop(1, nx, send_block, 0)
    anchors[pl.ds(sx, 1)] = block[...].reshape((1,) + block.shape)

    kept.wait()
    for g in range(staged):
        if g > 0:
            for more in range(staged + third * g, groups if g == staged - 1 else staged + third * (g + 1)):
                send_group(more)
        bunch = mid.at[pl.ds(0, width), pl.ds(0, ny - 1)]
        pltpu.make_async_copy(bunch, bunch, z_recv.at[g]).wait()
        for j in range(width):
            ox = group(g) + lax.rem(sx + j, width)
            if g == 0 and j == 0:
                pltpu.make_async_copy(mid.at[sx], got.at[sx], own.at[1]).start()
            else:
                remote(mid.at[ox], got.at[sx], near_send, near_recv, ox, sy).start()

    finish_eta()
    for k in range(layers):
        fill_rows(eta, (k,), [row_r[0, side, k : k + 1, :] for side in range(2)])
    loads[2 + nb].wait()
    icef = ice[0, 0].astype(F32)
    keep, gain = icef * (1.0 - RELAX), icef * RELAX

    def factor(i, carry):
        r = plain(i)
        for t in range(nb):
            last_up = last_ratio = None
            ratios = []
            for k in range(layers):
                centre = eta[k, t, at(i), :]
                before = eta[k, t - 1, at(i), :] if t > 0 else edge_tile(col_r.at[0], 0, i, k)
                after = eta[k, t + 1, at(i), :] if t < nb - 1 else edge_tile(col_r.at[0], 1, i, k)
                low, high = beside(lane, centre, before, after)
                w = 0.5 * (centre + eta[k, t, at(i, -1), :])
                e = 0.5 * (centre + eta[k, t, at(i, 1), :])
                s = 0.5 * (centre + low)
                n = 0.5 * (centre + high)
                pivot = w + e + s + n
                if k == 0:
                    pivot = pivot + fric[r, t * LANES : (t + 1) * LANES]
                if k < layers - 1:
                    up = centre + eta[k + 1, t, at(i), :]
                    pivot = pivot + up
                if k > 0:
                    pivot = pivot + last_up - last_up * last_ratio
                inverse = 1.0 / pivot
                west[k, t, r, :] = w * inverse
                east[k, t, r, :] = e * inverse
                south[k, t, r, :] = s * inverse
                north[k, t, r, :] = n * inverse
                if k > 0:
                    carry_c[k - 1, t, r, :] = last_up * inverse
                if k < layers - 1:
                    last_up, last_ratio = up, up * inverse
                    ratio_c[k, t, r, :] = last_ratio
                    ratios.append(last_ratio)
                else:
                    top_c[t, r, :] = inverse
                    unit = gain * inverse
            for k in range(layers - 1, -1, -1):
                if k < layers - 1:
                    unit = ratios[k] * unit
                coef[k, t, r, :] = unit
        return carry

    lax.fori_loop(0, blocks, factor, 0)

    pack_cols(1, single, lambda plane, t, i: coef[plane + (t, plain(i))])
    finish_coef = swap(1, [lambda t, r, k=k: coef[k, t, r : r + 1] for k in range(layers)])
    finish_coef()

    few = anchors.at[pl.ds(0, nx - 1)]
    pltpu.make_async_copy(few, few, small_recv.at[1]).wait()
    senders = nx * ny
    lookup[...] = jnp.transpose(anchors[...].astype(F32).reshape(senders, LANES))
    spot = lax.broadcasted_iota(jnp.int32, (nb * rows, senders), 0)
    band = jnp.zeros_like(spot)
    for t in range(1, nb):
        band = band + jnp.where(spot >= t * rows, 1, 0)
    spot = ((spot - band * rows) * nb + band).astype(F32)
    for load in loads[3 + nb :]:
        load.wait()
    far = got.at[pl.ds(0, (groups - staged) * width)]
    pltpu.make_async_copy(far, far, far_recv).wait()
    near = got.at[pl.ds(0, staged * width - 1)]
    pltpu.make_async_copy(near, near, near_recv).wait()
    pltpu.make_async_copy(mid.at[sx], got.at[sx], own.at[1]).wait()
    flat = got.reshape(senders * 3 * slots, LANES)
    for s in range(slots):
        row = lookup[pl.ds(s * nx + sx, 1), :]
        chosen = jnp.where(spot == row, 1.0, 0.0).astype(jnp.bfloat16)
        u, v, w = (flat[pl.ds(slots * c + s, senders, stride=3 * slots), :] for c in range(3))
        rest = jnp.concatenate([u * w, v * w, w], axis=1)
        high = rest.astype(jnp.bfloat16)
        rest = rest - high.astype(F32)
        middle = rest.astype(jnp.bfloat16)
        parts = jnp.concatenate([high, middle, (rest - middle.astype(F32)).astype(jnp.bfloat16)], axis=0)
        term = jnp.dot(jnp.concatenate([chosen] * 3, axis=1), parts, preferred_element_type=F32)
        if s == 0:
            total[...] = term
        else:
            total[...] += term
    for t in range(nb):
        part = slice(t * LANES, (t + 1) * LANES)
        weight = total[t * rows : (t + 1) * rows, 2 * LANES : 3 * LANES]
        for c in range(2):
            rhs[c, t] = weight * vel[c, :, part] - total[t * rows : (t + 1) * rows, c * LANES : (c + 1) * LANES]

    pack_cols(2, [(c,) for c in range(2)], lambda plane, t, i: rhs[plane + (t, plain(i))])
    finish_rhs = swap(2, [lambda t, r, c=c: rhs[c, t, r : r + 1] for c in range(2)])

    def first(i, carry):
        r = plain(i)
        for t in range(nb):
            drive = [rhs[c, t, r, :] for c in range(2)]
            for k in range(layers):
                unit = coef[k, t, r, :]
                for c in range(2):
                    adj_a[c, k, t, at(i), :] = unit * drive[c]
            for c in range(2):
                rhs[c, t, r, :] = drive[c] * top_c[t, r, :]
        return carry

    lax.fori_loop(0, blocks, first, 0)
    finish_rhs()
    for c in range(2):
        edges = [row_r[1, side, 0 : -(-layers // 8) * 8, :] * row_r[2, side, c : c + 1, :] for side in range(2)]
        for k in range(layers):
            fill_rows(adj_a, (c, k), [edge[k : k + 1, :] for edge in edges])

    def first_cols(i, carry):
        for side in range(2):
            unit = col_r[1, side, plain(i), :]
            drive = col_r[2, side, plain(i), :]
            unit = unit + pltpu.roll(unit, layers, 1)
            col_r[2, side, plain(i), :] = unit * jnp.where(lane < layers, drive[:, 0:1], drive[:, 1:2])
        return carry

    lax.fori_loop(0, blocks, first_cols, 0)

    def second(tiles_done):
        def sweep(i, carry):
            for t in tiles_done:
                def emit(c, k, made):
                    adj_b[c, k, t, at(i), :] = made

                solve(i, t, lane, nb, adj_a, col_r.at[2], (west, east, south, north), carry_c, ratio_c, rhs, keep, gain, emit)
            return carry

        return sweep

    planes = [(c, k) for c in range(2) for k in range(layers)]
    outer, inner = sorted({0, nb - 1}), list(range(1, nb - 1))
    lax.fori_loop(0, blocks, second(outer), 0)
    lax.fori_loop(0, 2, lambda i, carry: second(inner)(i * (blocks - 1), carry), 0)
    pack_cols(3, planes, lambda plane, t, i: adj_b[plane + (t, at(i))])
    finish_b = swap(3, [rows_in(adj_b, plane) for plane in planes])
    lax.fori_loop(1, blocks - 1, second(inner), 0)

    pltpu.make_async_copy(arrived, arrived, small_send.at[0]).wait()
    pltpu.make_async_copy(few, few, small_send.at[1]).wait()
    for g in range(staged):
        bunch = mid.at[pl.ds(0, width), pl.ds(0, ny - 1)]
        pltpu.make_async_copy(bunch, bunch, z_send.at[g]).wait()
    pltpu.make_async_copy(far, far, far_send).wait()
    pltpu.make_async_copy(near, near, near_send).wait()
    finish_b()
    for q, plane in enumerate(planes):
        fill_rows(adj_b, plane, [row_r[3, side, q : q + 1, :] for side in range(2)])


def last_sweep(pieces, adj_b, west, east, south, north, carry_c, ratio_c, rhs, cols_b, velocity, ice,
               out, gradient, made_v, grad_v, vel, load_sem, store_sem):
    layers, nb, rows = west.shape[0], west.shape[1], west.shape[2]
    loads = [pltpu.make_async_copy(velocity.at[c, 0], vel.at[c], load_sem.at[c]) for c in range(2)]
    for load in loads:
        load.start()
    lane = lax.broadcasted_iota(jnp.int32, (8, LANES), 1)
    icef = ice[0, 0].astype(F32)
    keep, gain = icef * (1.0 - RELAX), icef * RELAX

    def third(i, carry):
        r = plain(i)
        for t in range(nb):
            def emit(c, k, made):
                made_v[c, k, r, t * LANES : (t + 1) * LANES] = made

            solve(i, t, lane, nb, adj_b, cols_b, (west, east, south, north), carry_c, ratio_c, rhs, keep, gain, emit)
        return carry

    blocks = rows // 8
    each = -(-blocks // pieces)
    stores = []
    for p in range(0, blocks, each):
        stop = min(p + each, blocks)
        lax.fori_loop(p, stop, third, 0)
        some = pl.ds(p * 8, (stop - p) * 8)
        stores.append(pltpu.make_async_copy(made_v.at[:, :, some, :], out.at[:, :, some, :], store_sem.at[len(stores)]))
        stores[-1].start()
    for load in loads:
        load.wait()
    grad_v[...] = -icef * (made_v[0, 0] * vel[0] + made_v[1, 0] * vel[1])
    stores.append(pltpu.make_async_copy(grad_v, gradient, store_sem.at[len(stores)]))
    stores[-1].start()
    for store in stores:
        store.wait()


def per_device(nx, ny, velocity, viscosity, friction, ice_mask, obs_tiles, obs_cell, obs_count):
    comps, layers, rows, cols = velocity.shape
    slots, tile_len = obs_tiles.shape[4], obs_tiles.shape[6]
    nb = cols // tile_len
    width = max(1, nx // 8)
    staged, pieces = 2, 6
    in_vmem = pl.BlockSpec(memory_space=pltpu.VMEM)
    in_smem = pl.BlockSpec(memory_space=pltpu.SMEM)
    in_place = pl.BlockSpec(memory_space=pltpu.HBM)
    dma = pltpu.SemaphoreType.DMA

    tiles = obs_tiles.transpose(0, 1, 2, 3, 5, 4, 6).reshape(nx, ny, 3, slots, tile_len)
    cell = obs_cell.transpose(0, 1, 3, 4, 2).reshape(ny, slots, nx)
    count = obs_count.transpose(0, 1, 3, 2).reshape(ny, nx)
    halo_rows = rows + 2 * HALO
    packed = -(-comps * layers // 8) * 8
    face = pltpu.VMEM((layers, nb, rows, LANES), F32)
    link = pltpu.VMEM((layers - 1, nb, rows, LANES), F32)
    field = pltpu.VMEM((comps, layers, nb, halo_rows, LANES), F32)
    everyone = pltpu.VMEM((nx, ny, 3, slots, tile_len), F32)
    tiles, cell, count, velocity, viscosity, friction = (
        pltpu.with_memory_space_constraint(a, pltpu.HBM) for a in (tiles, cell, count, velocity, viscosity, friction)
    )
    state = pl.pallas_call(
        functools.partial(gather_and_sweep, nx, ny, width, staged),
        out_shape=(
            field, face, face, face, face, link, link,
            pltpu.VMEM((comps, nb, rows, LANES), F32),
            pltpu.VMEM((2, rows, LANES), F32),
        ),
        in_specs=[in_place] * 6 + [in_smem],
        out_specs=(in_vmem,) * 9,
        scratch_shapes=[
            pltpu.VMEM((layers, nb, halo_rows, LANES), F32),
            field,
            face,
            pltpu.VMEM((nb, rows, LANES), F32),
            pltpu.VMEM((comps, rows, cols), F32),
            pltpu.VMEM((rows, cols), F32),
            pltpu.VMEM((ny, slots, nx), jnp.int32),
            pltpu.VMEM((ny, nx), jnp.int32),
            everyone,
            everyone,
            pltpu.VMEM((ny, 1, LANES), jnp.int32),
            pltpu.VMEM((ny, 1, LANES), jnp.int32),
            pltpu.VMEM((ny, LANES), jnp.int32),
            pltpu.VMEM((nx, ny, LANES), jnp.int32),
            pltpu.VMEM((LANES, nx * ny), F32),
            pltpu.VMEM((nb * rows, 3 * LANES), F32),
            pltpu.VMEM((4, 2, packed, cols), F32),
            pltpu.VMEM((4, 2, packed, cols), F32),
            pltpu.VMEM((4, 2, rows, LANES), F32),
            pltpu.VMEM((3, 2, rows, LANES), F32),
            dma((nb + 5,)),
            dma((4, 4)),
            dma((4, 4)),
            pltpu.SemaphoreType.REGULAR,
            dma((staged,)),
            dma((staged,)),
            dma((2,)),
            dma, dma, dma, dma,
            dma((2,)),
            dma((2,)),
        ],
        compiler_params=pltpu.CompilerParams(collective_id=0, has_side_effects=True, vmem_limit_bytes=24 * 2**20),
        name="gather_and_sweep",
    )(tiles, cell, count, velocity, viscosity, friction, ice_mask)
    state = [pltpu.with_memory_space_constraint(a, pltpu.VMEM) for a in state]
    return pl.pallas_call(
        functools.partial(last_sweep, pieces),
        out_shape=(
            jax.ShapeDtypeStruct(velocity.shape, F32),
            jax.ShapeDtypeStruct((rows, cols), F32),
        ),
        in_specs=[in_vmem] * 9 + [in_place, in_smem],
        out_specs=(in_place, in_place),
        scratch_shapes=[
            pltpu.VMEM((comps, layers, rows, cols), F32),
            pltpu.VMEM((rows, cols), F32),
            pltpu.VMEM((comps, rows, cols), F32),
            dma((2,)),
            dma((pieces + 1,)),
        ],
        compiler_params=pltpu.CompilerParams(vmem_limit_bytes=16 * 2**20),
        name="last_sweep",
    )(*state, velocity, ice_mask)


def solution(mesh):
    placed = (
        P(None, None, "gx", "gy"),
        P(None, "gx", "gy"),
        P("gx", "gy"),
        P("gx", "gy"),
        P("gx", "gy", None, None, None, None, None),
        P("gx", "gy", None, None, None),
        P("gx", "gy", None, None),
    )
    return jax.shard_map(
        functools.partial(per_device, mesh.shape["gx"], mesh.shape["gy"]),
        mesh=mesh,
        in_specs=placed,
        out_specs=(P(None, None, "gx", "gy"), P("gx", "gy")),
        check_vma=False,
    )
```
